512 devices in a mesh: dp: 16 (over y, x), expert: 32 (over z, core).
Axes of the slice: x: 4, y: 4, z: 16, core: 2. Of those that a mesh axis runs over, the one named last changes fastest.
Arguments:
- tokens: bfloat16 [65536, 1024], P(('dp', 'expert')), may hold values from -6 to 6
- cotangent: bfloat16 [65536, 1024], P(('dp', 'expert')), may hold values from -4 to 4
- expert_ids: int32 [65536, 8], P(('dp', 'expert')), may hold values from 0 to 63, all different within a row; in each aligned block of 128 rows (0 to 127, 128 to 255, ...) at most 21 rows name the same one
- gate_weights: bfloat16 [65536, 8], P(('dp', 'expert')), may hold values from 0.19921875 to 1
- up_weight: bfloat16 [64, 1024, 384], P('expert'), may hold values from -0.1875 to 0.1875
- up_adapter_first: bfloat16 [64, 1024, 16], P('expert'), may hold values from -0.1875 to 0.1875
- up_adapter_second: bfloat16 [64, 16, 384], P('expert'), may hold values from -0.375 to 0.375
- down_weight: bfloat16 [64, 384, 1024], P('expert'), may hold values from -0.3125 to 0.3125
- down_adapter_first: bfloat16 [64, 384, 16], P('expert'), may hold values from -0.3125 to 0.3125
- down_adapter_second: bfloat16 [64, 16, 1024], P('expert'), may hold values from -0.375 to 0.375
Outputs:
- input_grad: bfloat16 [65536, 1024], P(('dp', 'expert'))
- gate_grad: bfloat16 [65536, 8], P(('dp', 'expert'))
- up_first_gradient: bfloat16 [64, 1024, 16], P('expert')
- up_second_gradient: bfloat16 [64, 16, 384], P('expert')
- down_first_gradient: bfloat16 [64, 384, 16], P('expert')
- down_second_gradient: bfloat16 [64, 16, 1024], P('expert')
The draws below stay inside these ranges and needn't reach their ends.
Inputs may be any that keep to these rules, and one draw needn't show every extreme that they name: `expert_ids`: in each device's block of 128 tokens no expert is named more than 21 times, a bound that some block reaches; a token's 8 experts differ.
All inputs are finite; a program needn't handle non-finite values.
Results may differ from the reference program's by a relative error of at most 0.015.
Values may be sent and summed in bfloat16 or wider, within the bound.
A program may use at most 64 MiB of HBM per device.

```python
import math
import jax
import jax.numpy as jnp
import numpy as np
from jax import lax

D = 1024
FF = 384
R = 16
TOP = 8
TOK_DEV = 128
EXPERTS = 64
CAP = 21
GROUP_ROWS = 4096
TOKENS = 65536
N_DP = 16
N_EXPERT = 32


def levels(stream_key, shape, cuts, smallest, high):
    factor_of, own = 1.0, jax.random.fold_in(stream_key, 6)
    for dim, parts in cuts:
        draws = jnp.exp(jax.random.uniform(jax.random.fold_in(own, dim), (parts,), jnp.float32, smallest / len(cuts), high / len(cuts)))
        factor_of = factor_of * jnp.repeat(draws, shape[dim] // parts).reshape([-1 if axis == dim else 1 for axis in range(len(shape))])
    return factor_of


def routed_block(own_key, own, number, rows, amount, top, reach, slope):
    order = jax.random.permutation(own_key, amount)
    heavy_load, common = load_shares(amount, rows * top, reach, slope, True), load_shares(amount, rows * top, reach, slope, False)
    places = jnp.arange(amount)

    def named(sizes, turn):
        used = int((sizes > 0).sum())
        fixed = max(1, used // 4)
        shifted = fixed + (places - fixed + turn * (used - fixed)) % max(1, amount - fixed)
        return jnp.zeros((amount,), jnp.int32).at[order[jnp.where(places < fixed, places, shifted)]].set(jnp.asarray(sizes, jnp.int32))

    sizes = jnp.where(number % 4 == 0, named(heavy_load, number // 4), named(common, number - number // 4 - 1))
    mixed = jax.random.permutation(jax.random.fold_in(own, 3), amount)
    donor, sink = mixed[0:amount // 2 * 2:2], mixed[1:amount // 2 * 2:2]
    room = jnp.minimum(sizes[donor] - 1, reach - sizes[sink]) // 2
    room = jnp.where((donor == order[0]) | (sink == order[0]) | (sizes[sink] == 0), 0, jnp.maximum(room, 0))
    shifted = jax.random.randint(jax.random.fold_in(own, 4), (amount // 2,), 0, 1 << 20) % (room + 1)
    sizes = sizes.at[donor].add(-shifted).at[sink].add(shifted)
    labels = jnp.searchsorted(jnp.cumsum(sizes), jnp.arange(rows * top), side="right").astype(jnp.int32)
    grid = labels.reshape(top, rows).T
    grid = grid[jax.random.permutation(jax.random.fold_in(own, 1), rows)]
    turn = jax.random.randint(jax.random.fold_in(own, 2), (rows, 1), 0, top)
    return jnp.take_along_axis(grid, (jnp.arange(top)[None, :] + turn) % top, axis=1)


def load_shares(amount, total, reach, slope, full):
    loads = [(1 << 20) // math.isqrt(grade ** slope) + 1 for grade in range(1, amount + 1)]
    largest = reach if full else min(reach, max(-(-total // amount), total * loads[0] // sum(loads)))
    least = 1 if total - largest >= amount - 1 else 0
    given, rest = [largest] + [least] * (amount - 1), total - largest - least * (amount - 1)
    while rest > 0:
        free = [i for i in range(1, amount) if given[i] < largest] or [i for i in range(1, amount) if given[i] < reach]
        whole, remaining = sum([loads[i] for i in free]), rest
        for i in free:
            addition = min(reach - given[i], max(1, remaining * loads[i] // whole), rest)
            given[i] = given[i] + addition
            rest = rest - addition
    return np.array(given)


def bell_draw(own_key, dims, width, limit, cuts=(), kind=jnp.bfloat16):
    level = levels(own_key, dims, cuts, -0.22, 0.18) if cuts else 1.0
    entries = jax.random.normal(own_key, dims, jnp.float32) * width * level
    return jnp.minimum(jnp.maximum(entries, -limit), limit).astype(kind)


def setup_inputs(seed: int = 0) -> dict:
    keys = jax.random.split(jax.random.key(seed), 11)
    tokens = bell_draw(keys[0], (TOKENS, D), 1.0, 6.0, ((0, 512),))
    cotangent = bell_draw(keys[1], (TOKENS, D), 0.25, 4.0, ((0, 512),))
    expert_ids_keys = jax.random.split(jax.random.fold_in(keys[2], 1), TOKENS // TOK_DEV)
    expert_ids_turns = jax.random.permutation(jax.random.fold_in(keys[2], 3), TOKENS // TOK_DEV)
    expert_ids = jax.vmap(lambda own, number: routed_block(jax.random.fold_in(keys[2], 2), own, number, TOK_DEV, EXPERTS, TOP, CAP, 2))(expert_ids_keys, expert_ids_turns).reshape((TOKENS, TOP))
    gate_weights = jnp.clip(0.19921875 + 0.80078125 * jax.random.uniform(keys[3], (TOKENS, TOP), jnp.float32) ** levels(keys[3], (TOKENS, TOP), ((0, 512),), -0.2, 0.2), 0.19921875, 1.0).astype(jnp.bfloat16)
    up_weight = bell_draw(keys[4], (EXPERTS, D, FF), D ** -0.5, 0.1875, ((0, 32),))
    up_adapter_first = bell_draw(keys[5], (EXPERTS, D, R), D ** -0.5, 0.1875, ((0, 32),))
    up_adapter_second = bell_draw(keys[6], (EXPERTS, R, FF), (16 * R) ** -0.5, 0.375, ((0, 32),))
    down_weight = bell_draw(keys[7], (EXPERTS, FF, D), FF ** -0.5, 0.3125, ((0, 32),))
    down_adapter_first = bell_draw(keys[8], (EXPERTS, FF, R), FF ** -0.5, 0.3125, ((0, 32),))
    down_adapter_second = bell_draw(keys[9], (EXPERTS, R, D), (16 * R) ** -0.5, 0.375, ((0, 32),))
    return dict(tokens=tokens, cotangent=cotangent, expert_ids=expert_ids, gate_weights=gate_weights, up_weight=up_weight, up_adapter_first=up_adapter_first, up_adapter_second=up_adapter_second, down_weight=down_weight, down_adapter_first=down_adapter_first, down_adapter_second=down_adapter_second)


adapter_scale = 2.0


def slot_numbers(flat_ids, experts_all):
    onehot = (flat_ids[..., None] == jnp.arange(experts_all, dtype=jnp.int32)).astype(jnp.int32)
    before = jnp.cumsum(onehot, axis=-2) - onehot
    return jnp.sum(before * onehot, axis=-1).astype(jnp.int32)


def silu_slope(preactivation):
    sigmoid_val = jax.nn.sigmoid(preactivation)
    return sigmoid_val * (1.0 + preactivation * (1.0 - sigmoid_val))


def tensor_contraction(first_op, second_op, pattern):
    return jnp.einsum(pattern, first_op.astype(jnp.float32), second_op.astype(jnp.float32))


def reference(tokens, cotangent, expert_ids, gate_weights, up_weight, up_adapter_first, up_adapter_second, down_weight, down_adapter_first, down_adapter_second):
    n_slots = EXPERTS * N_EXPERT * CAP

    def one_group(pieces):
        grp_tokens, grp_cot, grp_ids, grp_gates = pieces
        block_ids = grp_ids.reshape(N_EXPERT, TOK_DEV * TOP)
        slot_index = slot_numbers(block_ids, EXPERTS)
        source = jnp.arange(N_EXPERT, dtype=jnp.int32)[:, None]
        target = ((block_ids * N_EXPERT + source) * CAP + slot_index).reshape(-1).astype(jnp.int32)
        owners = jnp.arange(GROUP_ROWS * TOP, dtype=jnp.int32) // TOP
        token_of = jnp.zeros((n_slots,), jnp.int32).at[target].set(owners)
        filled = jnp.zeros((n_slots,), jnp.int32).at[target].set(1) > 0
        input_rows = jnp.where(filled[:, None], grp_tokens[token_of], 0).reshape(EXPERTS, N_EXPERT * CAP, D)
        cot_rows = jnp.where(filled[:, None], grp_cot[token_of], 0).reshape(EXPERTS, N_EXPERT * CAP, D)
        gate_rows = jnp.zeros((n_slots,), grp_gates.dtype).at[target].set(grp_gates.reshape(-1))
        gate_rows = gate_rows.reshape(EXPERTS, N_EXPERT * CAP)
        up_low_rank = tensor_contraction(input_rows, up_adapter_first, "ecd,edr->ecr").astype(jnp.bfloat16)
        preactivation = tensor_contraction(input_rows, up_weight, "jqb,jbn->jqn") + adapter_scale * tensor_contraction(up_low_rank, up_adapter_second, "uhd,uds->uhs")
        hidden_units = jax.nn.silu(preactivation).astype(jnp.bfloat16)
        down_low_rank = tensor_contraction(hidden_units, down_adapter_first, "ecf,efr->ecr").astype(jnp.bfloat16)
        output_rows = tensor_contraction(hidden_units, down_weight, "yxz,yzh->yxh") + adapter_scale * tensor_contraction(down_low_rank, down_adapter_second, "xom,xmi->xoi")
        slot_gate = jnp.sum(output_rows * cot_rows.astype(jnp.float32), axis=-1).astype(jnp.bfloat16)
        scaled_rows = (gate_rows.astype(jnp.float32)[..., None] * cot_rows.astype(jnp.float32)).astype(jnp.bfloat16)
        down_low_rank_gradient = tensor_contraction(scaled_rows, down_adapter_second, "ecd,erd->ecr").astype(jnp.bfloat16)
        hidden_gradient = tensor_contraction(scaled_rows, down_weight, "pvr,ptr->pvt") + adapter_scale * tensor_contraction(down_low_rank_gradient, down_adapter_first, "snk,sok->sno")
        preactivation_gradient = (hidden_gradient * silu_slope(preactivation)).astype(jnp.bfloat16)
        up_low_rank_gradient = tensor_contraction(preactivation_gradient, up_adapter_second, "ecf,erf->ecr").astype(jnp.bfloat16)
        row_gradient = tensor_contraction(preactivation_gradient, up_weight, "wvb,wqb->wvq") + adapter_scale * tensor_contraction(up_low_rank_gradient, up_adapter_first, "xyj,xfj->xyf")
        row_gradient = row_gradient.astype(jnp.bfloat16)
        up_first_gradient = adapter_scale * tensor_contraction(input_rows, up_low_rank_gradient, "jbn,jbs->jns")
        up_second_gradient = adapter_scale * tensor_contraction(up_low_rank, preactivation_gradient, "bil,bit->blt")
        down_first_gradient = adapter_scale * tensor_contraction(hidden_units, down_low_rank_gradient, "jly,jli->jyi")
        down_second_gradient = adapter_scale * tensor_contraction(down_low_rank, scaled_rows, "onl,onk->olk")
        picked = row_gradient.reshape(n_slots, D)[target].astype(jnp.float32).reshape(GROUP_ROWS, TOP, D)
        input_grad = jnp.sum(picked, axis=1).astype(jnp.bfloat16)
        gate_grad = slot_gate.reshape(-1)[target].reshape(GROUP_ROWS, TOP)
        return input_grad, gate_grad, up_first_gradient, up_second_gradient, down_first_gradient, down_second_gradient

    results = lax.map(one_group, (tokens.reshape(N_DP, GROUP_ROWS, D), cotangent.reshape(N_DP, GROUP_ROWS, D),
                                  expert_ids.reshape(N_DP, GROUP_ROWS, TOP), gate_weights.reshape(N_DP, GROUP_ROWS, TOP)))
    return (results[0].reshape(TOKENS, D), results[1].reshape(TOKENS, TOP),
            jnp.sum(results[2], axis=0).astype(jnp.bfloat16), jnp.sum(results[3], axis=0).astype(jnp.bfloat16),
            jnp.sum(results[4], axis=0).astype(jnp.bfloat16), jnp.sum(results[5], axis=0).astype(jnp.bfloat16))
```

```python
import functools

import jax
import jax.numpy as jnp
from jax import lax
from jax.experimental import pallas as pl
from jax.experimental.pallas import tpu as pltpu
from jax.sharding import PartitionSpec as P

adapter_scale = 2.0
PIECE_BLOCKS = 2
SLOTS = 48


def mm(a, b, dims):
    return lax.dot_general(a, b, (dims, ((), ())), preferred_element_type=jnp.float32)


def bmm(pattern, a, b):
    return jnp.einsum(pattern, a, b, preferred_element_type=jnp.float32)


NN = ((1,), (0,))
NT = ((1,), (1,))
TN = ((0,), (0,))


def dma(src, dst, send, recv, axis, index):
    return pltpu.make_async_remote_copy(
        src_ref=src,
        dst_ref=dst,
        send_sem=send,
        recv_sem=recv,
        device_id={axis: index},
        device_id_type=pl.DeviceIdType.MESH,
    )


def greet(axis, peers):
    barrier = pltpu.get_barrier_semaphore()
    for peer in peers:
        pl.semaphore_signal(
            barrier, inc=1, device_id={axis: peer}, device_id_type=pl.DeviceIdType.MESH
        )
    pl.semaphore_wait(barrier, len(peers))


def ring_place(n):
    me = lax.axis_index("expert")
    z, core = me // 2, lax.rem(me, 2)
    at = lambda off: lax.rem(z + off + 2 * n, n)
    return me, z, core, at


def ring_chains(n, tensors):
    far, near = n // 2, n - 1 - n // 2
    chains = []
    for t in range(tensors):
        chains.append((t, 1, far if t != 1 else near))
        chains.append((t, -1, near if t != 1 else far))
    return chains


def gather_kernel(n, x, c, m, xo, co, mo, send, recv, psend, precv, own):
    me, z, core, at = ring_place(n)
    mate = z * 2 + 1 - core
    greet("expert", [at(1) * 2 + core, at(-1) * 2 + core, mate])
    ins, outs = (x, c, m), (xo, co, mo)
    chains = ring_chains(n, 3)
    ring, pair, local = {}, [], []

    def to_mate(t, k, src, block):
        copy = dma(src, outs[t].at[block], psend.at[t, k], precv.at[t, k], "expert", mate)
        copy.start()
        pair.append(copy)

    for s in range(n // 2 + 1):
        for ci, (t, d, hops) in enumerate(chains):
            block = at(-d * s) * 2 + core
            if 0 < s <= hops:
                ring[ci, s - 1].wait_recv()
            if s < hops:
                src = ins[t] if s == 0 else outs[t].at[block]
                ring[ci, s] = dma(
                    src, outs[t].at[block], send.at[ci, s], recv.at[ci, s],
                    "expert", at(d) * 2 + core,
                )
                ring[ci, s].start()
            if 0 < s <= hops:
                to_mate(t, s if d > 0 else n - s, outs[t].at[block], block)
        if s == 0:
            for t in range(3):
                to_mate(t, 0, ins[t], me)
                copy = pltpu.make_async_copy(ins[t], outs[t].at[me], own.at[t])
                copy.start()
                local.append(copy)
    for copy in ring.values():
        copy.wait_send()
    for copy in pair:
        copy.wait()
    for copy in local:
        copy.wait()


def gather_rows(x, c, m, n_dev):
    n = n_dev // 2
    dma_sem = pltpu.SemaphoreType.DMA
    return pl.pallas_call(
        functools.partial(gather_kernel, n),
        out_shape=[jax.ShapeDtypeStruct((n_dev,) + a.shape, a.dtype) for a in (x, c, m)],
        in_specs=[pl.BlockSpec(memory_space=pltpu.VMEM)] * 3,
        out_specs=[pl.BlockSpec(memory_space=pl.ANY)] * 3,
        scratch_shapes=[
            dma_sem((6, n // 2)),
            dma_sem((6, n // 2)),
            dma_sem((3, n)),
            dma_sem((3, n)),
            dma_sem((3,)),
        ],
        compiler_params=pltpu.CompilerParams(collective_id=0, has_side_effects=True),
    )(x, c, m)


def scatter_kernel(n, part, gate, out, gout, mp, mg, sa, ra, sb, rb, sg, rg, send, recv, psend, precv):
    me, z, core, at = ring_place(n)
    mate = z * 2 + 1 - core
    half = part.shape[1] // 2
    greet("expert", [at(1) * 2 + core, at(-1) * 2 + core, mate])
    chains = ring_chains(n, 3)
    rows = (pl.ds(0, half), pl.ds(half, half), slice(None))
    sends, recvs = (sa, sb, sg), (ra, rb, rg)
    ring = {}

    order = [n // 2]
    for k in range(n // 2 - 1, 0, -1):
        order += [k, n - k]
    order.append(0)
    gcopy = dma(gate.at[1 - core], mg, psend.at[n], precv.at[n], "expert", mate)
    gcopy.start()
    pair = {}
    for k in order:
        pair[k] = dma(
            part.at[at(k) * 2 + 1 - core], mp.at[at(k)], psend.at[k], precv.at[k], "expert", mate
        )
        pair[k].start()
    arrived = set()

    def mine(t, k):
        if t == 2:
            if "g" not in arrived:
                gcopy.wait_recv()
                arrived.add("g")
            return gate[core, at(k)].astype(jnp.float32) + mg[at(k)].astype(jnp.float32)
        if k not in arrived:
            pair[k].wait_recv()
            arrived.add(k)
        return part[at(k) * 2 + core, rows[t]].astype(jnp.float32) + mp[at(k), rows[t]].astype(
            jnp.float32
        )

    for s in range(n // 2):
        for ci, (t, d, hops) in enumerate(chains):
            if s >= hops:
                continue
            total = mine(t, (d * (hops - s)) % n)
            slot = 0 if d > 0 else 1
            if s > 0:
                ring[ci, s - 1].wait_recv()
                total = total + recvs[t][slot, s - 1].astype(jnp.float32)
            sends[t][slot, s] = total.astype(jnp.bfloat16)
            ring[ci, s] = dma(
                sends[t].at[slot, s], recvs[t].at[slot, s], send.at[ci, s], recv.at[ci, s],
                "expert", at(d) * 2 + core,
            )
            ring[ci, s].start()
    for t in range(3):
        total = mine(t, 0)
        for ci, (u, d, hops) in enumerate(chains):
            if u == t:
                ring[ci, hops - 1].wait_recv()
                total = total + recvs[t][0 if d > 0 else 1, hops - 1].astype(jnp.float32)
        if t == 2:
            gout[...] = total.astype(jnp.bfloat16)
        else:
            out[rows[t]] = total.astype(jnp.bfloat16)
    for copy in ring.values():
        copy.wait_send()
    for copy in pair.values():
        copy.wait_send()
    gcopy.wait_send()


def scatter_rows(part, gate):
    n_dev, rows, width = part.shape
    n = n_dev // 2
    bf = jnp.bfloat16
    gshape = gate.shape[2:]
    dma_sem = pltpu.SemaphoreType.DMA
    return pl.pallas_call(
        functools.partial(scatter_kernel, n),
        out_shape=[
            jax.ShapeDtypeStruct((rows, width), bf),
            jax.ShapeDtypeStruct(gshape, bf),
        ],
        in_specs=[pl.BlockSpec(memory_space=pltpu.VMEM)] * 2,
        out_specs=[pl.BlockSpec(memory_space=pltpu.VMEM)] * 2,
        scratch_shapes=[
            pltpu.VMEM((n, rows, width), bf),
            pltpu.VMEM((n,) + gshape, bf),
            pltpu.VMEM((2, n // 2, rows // 2, width), bf),
            pltpu.VMEM((2, n // 2, rows // 2, width), bf),
            pltpu.VMEM((2, n // 2, rows // 2, width), bf),
            pltpu.VMEM((2, n // 2, rows // 2, width), bf),
            pltpu.VMEM((2, n // 2) + gshape, bf),
            pltpu.VMEM((2, n // 2) + gshape, bf),
            dma_sem((6, n // 2)),
            dma_sem((6, n // 2)),
            dma_sem((n + 1,)),
            dma_sem((n + 1,)),
        ],
        compiler_params=pltpu.CompilerParams(
            collective_id=1, has_side_effects=True, vmem_limit_bytes=48 * 1024 * 1024
        ),
    )(part, gate)


def sum_kernel(n, flat, out, got, mine, send, recv, send2, recv2):
    me = lax.axis_index("dp")
    at = lambda off: lax.rem(me + off + n, n)
    greet("dp", [at(k) for k in range(1, n)])
    first, second = [], []
    for k in range(1, n):
        first.append(
            dma(flat.at[at(k)], got.at[k], send.at[k], recv.at[k], "dp", at(k))
        )
        first[-1].start()
    total = flat[me]
    for k in range(1, n):
        first[k - 1].wait_recv()
        total = total + got[k]
    mine[...] = total.astype(mine.dtype)
    for k in range(1, n):
        second.append(dma(mine, out.at[me], send2.at[k], recv2.at[k], "dp", at(k)))
        second[-1].start()
    out[me] = total.astype(mine.dtype)
    for copy in first:
        copy.wait_send()
    for copy in second:
        copy.wait()


def sum_groups(flat):
    n = flat.shape[0]
    dma_sem = pltpu.SemaphoreType.DMA
    return pl.pallas_call(
        functools.partial(sum_kernel, n),
        out_shape=jax.ShapeDtypeStruct(flat.shape, jnp.bfloat16),
        in_specs=[pl.BlockSpec(memory_space=pltpu.VMEM)],
        out_specs=pl.BlockSpec(memory_space=pltpu.VMEM),
        scratch_shapes=[
            pltpu.VMEM(flat.shape, jnp.float32),
            pltpu.VMEM(flat.shape[1:], jnp.bfloat16),
            dma_sem((n,)),
            dma_sem((n,)),
            dma_sem((n,)),
            dma_sem((n,)),
        ],
        compiler_params=pltpu.CompilerParams(collective_id=2, has_side_effects=True),
    )(flat)


def shards(tokens, cotangent, expert_ids, gate_weights, up_w, up_a, up_b, dn_w, dn_a, dn_b):
    bf = jnp.bfloat16
    f32 = jnp.float32
    n_dev = lax.axis_size("expert")
    n_dp = lax.axis_size("dp")
    local = up_w.shape[0]
    rows, width = tokens.shape
    ff = up_w.shape[2]
    rank = up_a.shape[2]
    top = expert_ids.shape[1]
    piece = PIECE_BLOCKS * rows
    n_piece = n_dev // PIECE_BLOCKS
    me = lax.axis_index("expert")

    meta = jnp.concatenate([expert_ids.T.astype(bf), gate_weights.T], axis=0)
    x_all, c_all, meta = gather_rows(tokens, cotangent, meta, n_dev)
    x_all = x_all.reshape(n_piece, piece, width)
    c_all = c_all.reshape(n_piece, piece, width)

    ids = meta[:, :top, :].astype(jnp.int32)
    gates = meta[:, top:, :].astype(f32)
    before = (
        lax.broadcasted_iota(jnp.int32, (piece, piece), 0)
        < lax.broadcasted_iota(jnp.int32, (piece, piece), 1)
    ).astype(bf)
    hits, picks, gate_rows = [], [], []
    for j in range(local):
        hit = (ids == me * local + j).astype(f32)
        mask = jnp.sum(hit, axis=1).reshape(n_piece, piece)
        gate = jnp.sum(hit * gates, axis=1).reshape(n_piece, 1, piece)
        place = mm(mask.astype(bf), before, NN).reshape(n_piece, 1, piece)
        slot = lax.broadcasted_iota(jnp.int32, (n_piece, SLOTS, piece), 1).astype(f32)
        pick = jnp.where(slot == place, mask.reshape(n_piece, 1, piece), 0.0)
        gate_rows.append(jnp.sum(pick * gate, axis=2).reshape(n_piece * SLOTS, 1))
        picks.append(pick.astype(bf))
        hits.append(hit)

    forward = []
    for j in range(local):
        x = bmm("gst,gtd->gsd", picks[j], x_all).astype(bf).reshape(n_piece * SLOTS, width)
        low_up = mm(x, up_a[j], NN).astype(bf)
        pre = mm(x, up_w[j], NN) + adapter_scale * mm(low_up, up_b[j], NN)
        hidden = jax.nn.silu(pre).astype(bf)
        low_dn = mm(hidden, dn_a[j], NN).astype(bf)
        forward.append((x, low_up, pre, hidden, low_dn))

    gate_out = 0.0
    row_grads, adapters = [], []
    for j in range(local):
        x, low_up, pre, hidden, low_dn = forward[j]
        c = bmm("gst,gtd->gsd", picks[j], c_all).astype(bf).reshape(n_piece * SLOTS, width)
        cf = c.astype(f32)
        out = mm(hidden, dn_w[j], NN) + adapter_scale * mm(low_dn, dn_b[j], NN)
        slot_gate = jnp.sum(out * cf, axis=1).astype(bf).astype(f32)
        back = jnp.sum(picks[j].astype(f32) * slot_gate.reshape(n_piece, SLOTS, 1), axis=1)
        gate_out += hits[j] * back.reshape(n_dev, 1, rows)
        scaled = (gate_rows[j] * cf).astype(bf)
        lg_dn = mm(scaled, dn_b[j], NT).astype(bf)
        hg = mm(scaled, dn_w[j], NT) + adapter_scale * mm(lg_dn, dn_a[j], NT)
        s = jax.nn.sigmoid(pre)
        pg = (hg * (s * (1.0 + pre * (1.0 - s)))).astype(bf)
        lg_up = mm(pg, up_b[j], NT).astype(bf)
        rg = (mm(pg, up_w[j], NT) + adapter_scale * mm(lg_up, up_a[j], NT)).astype(bf)
        row_grads.append(rg.reshape(n_piece, SLOTS, width))
        adapters.append(
            (
                adapter_scale * mm(lg_up, x, TN),
                adapter_scale * mm(low_up, pg, TN),
                adapter_scale * mm(lg_dn, hidden, TN),
                adapter_scale * mm(low_dn, scaled, TN),
            )
        )
    part = bmm(
        "gst,gsd->gtd", jnp.concatenate(picks, axis=1), jnp.concatenate(row_grads, axis=1)
    ).astype(bf)
    gate_out = gate_out.astype(bf).reshape(n_dev // 2, 2, top, rows).swapaxes(0, 1)
    gate_out = jnp.pad(gate_out, ((0, 0), (0, 0), (0, 16 - top), (0, 0)))
    input_grad, gate_grad = scatter_rows(part.reshape(n_dev, rows, width), gate_out)
    gate_grad = gate_grad[:top].T

    flat = jnp.stack([jnp.concatenate(a, axis=1) for a in adapters])
    cols = flat.shape[2]
    full = sum_groups(flat.reshape(n_dp, -1, 128)).reshape(local, rank, cols)
    au, bu, ad, bd = jnp.split(full, [width, width + ff, width + 2 * ff], axis=2)
    return (
        input_grad,
        gate_grad,
        au.transpose(0, 2, 1),
        bu,
        ad.transpose(0, 2, 1),
        bd,
    )


def solution(mesh):
    rows = P(("dp", "expert"), None)
    experts = P("expert", None, None)
    return jax.shard_map(
        shards,
        mesh=mesh,
        in_specs=(rows,) * 4 + (experts,) * 6,
        out_specs=(rows,) * 2 + (experts,) * 4,
        check_vma=False,
    )
```

```python
import functools

import jax
import jax.numpy as jnp
from jax import lax
from jax.experimental import pallas as pl
from jax.experimental.pallas import tpu as pltpu
from jax.sharding import PartitionSpec as P

adapter_scale = 2.0
PIECE_BLOCKS = 2
SLOTS = 48


def mm(a, b, dims):
    return lax.dot_general(a, b, (dims, ((), ())), preferred_element_type=jnp.float32)


NN = ((1,), (0,))
NT = ((1,), (1,))
TN = ((0,), (0,))


def dma(src, dst, send, recv, axis, index):
    return pltpu.make_async_remote_copy(
        src_ref=src,
        dst_ref=dst,
        send_sem=send,
        recv_sem=recv,
        device_id={axis: index},
        device_id_type=pl.DeviceIdType.MESH,
    )


def greet(peers):
    barrier = pltpu.get_barrier_semaphore()
    for axis, peer in peers:
        pl.semaphore_signal(
            barrier, inc=1, device_id={axis: peer}, device_id_type=pl.DeviceIdType.MESH
        )
    pl.semaphore_wait(barrier, len(peers))


def ring_place(n):
    me = lax.axis_index("expert")
    z, core = me // 2, lax.rem(me, 2)
    at = lambda off: lax.rem(z + off + 2 * n, n)
    return me, z, core, at


def ring_chains(n, tensors):
    far, near = n // 2, n - 1 - n // 2
    chains = []
    for t in range(tensors):
        chains.append((t, 1, far if t != 1 else near))
        chains.append((t, -1, near if t != 1 else far))
    return chains


def step_kernel(n, n_dp, top, x, c, m, up_w, up_a, up_b, dn_w, dn_a, dn_b, out, gout, summed,
                xo, co, mo, before, part, gate, mp, mg, sa, ra, sb, rb, sg, rg, acc, got, added,
                gsend, grecv, gpsend, gprecv, own, send, recv, psend, precv, send1, recv1, send2, recv2):
    bf, f32 = jnp.bfloat16, jnp.float32
    me, z, core, at = ring_place(n)
    mate = z * 2 + 1 - core
    group = lax.axis_index("dp")
    gat = lambda off: lax.rem(group + off + n_dp, n_dp)
    greet(
        [("expert", at(1) * 2 + core), ("expert", at(-1) * 2 + core), ("expert", mate)]
        + [("dp", gat(k)) for k in range(1, n_dp)]
    )
    chains = ring_chains(n, 3)
    local = up_w.shape[0]
    rows, width = x.shape
    piece = PIECE_BLOCKS * rows

    ins, outs = (x, c, m), (xo, co, mo)

    def hop(ci, s, first=False):
        t, d, _ = chains[ci]
        block = at(-d * s) * 2 + core
        return dma(
            ins[t] if first else outs[t].at[block], outs[t].at[block],
            gsend.at[ci, s], grecv.at[ci, s], "expert", at(d) * 2 + core,
        )

    def to_mate(ci, s):
        t, d, _ = chains[ci]
        block = at(-d * s) * 2 + core
        return dma(
            outs[t].at[block], outs[t].at[block],
            gpsend.at[ci, s], gprecv.at[ci, s], "expert", mate,
        )

    def own_to_mate(t):
        return dma(ins[t], outs[t].at[me], gpsend.at[2 * t, 0], gprecv.at[2 * t, 0], "expert", mate)

    def own_copy(t):
        return pltpu.make_async_copy(ins[t], outs[t].at[me], own.at[t])

    def move(s, active, forward):
        for ci in active:
            hop(ci, s - 1).wait_recv()
            if ci in forward:
                hop(ci, s).start()
            to_mate(ci, s).start()

    def reach(s):
        return [ci for ci, (_, _, hops) in enumerate(chains) if hops >= s]

    def compute(pieces):
        picks, hits, gate_rows = {}, {}, {}
        blocks = {}
        for i, p in enumerate(pieces):
            blocks[i] = [mo[2 * p + b].astype(f32) for b in range(2)]
            for j in range(local):
                e = (me * local + j).astype(f32)
                hits[i, j] = [(v[:top] == e).astype(f32) for v in blocks[i]]
                mask = jnp.concatenate(
                    [jnp.sum(h, axis=0, keepdims=True) for h in hits[i, j]], axis=1
                )
                weight = jnp.concatenate(
                    [
                        jnp.sum(h * v[top : 2 * top], axis=0, keepdims=True)
                        for h, v in zip(hits[i, j], blocks[i])
                    ],
                    axis=1,
                )
                place = mm(jnp.broadcast_to(mask, (8, piece)).astype(bf), before[...], NN)[:1]
                slot = lax.broadcasted_iota(jnp.int32, (SLOTS, piece), 0).astype(f32)
                pick = jnp.where(slot == place, jnp.broadcast_to(mask, (SLOTS, piece)), 0.0)
                gate_rows[i, j] = jnp.sum(pick * weight, axis=1, keepdims=True)
                picks[i, j] = pick
        grads = {}
        gates = [[0.0, 0.0] for _ in pieces]

        def take(source, j):
            return jnp.concatenate(
                [
                    mm(picks[i, j].astype(bf), source[pl.ds(2 * p, 2)].reshape(piece, width), NN)
                    for i, p in enumerate(pieces)
                ],
                axis=0,
            )

        for j in range(local):
            xr = take(xo, j).astype(bf)
            cf = take(co, j)
            low_up = mm(xr, up_a[j], NN).astype(bf)
            pre = mm(xr, up_w[j], NN) + adapter_scale * mm(low_up, up_b[j], NN)
            s = jax.nn.sigmoid(pre)
            hidden = (pre * s).astype(bf)
            low_dn = mm(hidden, dn_a[j], NN).astype(bf)
            res = mm(hidden, dn_w[j], NN) + adapter_scale * mm(low_dn, dn_b[j], NN)
            slot_gate = jnp.sum(res * cf, axis=1, keepdims=True).astype(bf).astype(f32)
            weight = jnp.concatenate([gate_rows[i, j] for i in range(len(pieces))], axis=0)
            scaled = (weight * cf).astype(bf)
            lg_dn = mm(scaled, dn_b[j], NT).astype(bf)
            hg = mm(scaled, dn_w[j], NT) + adapter_scale * mm(lg_dn, dn_a[j], NT)
            pg = (hg * (s * (1.0 + pre * (1.0 - s)))).astype(bf)
            lg_up = mm(pg, up_b[j], NT).astype(bf)
            rg = (mm(pg, up_w[j], NT) + adapter_scale * mm(lg_up, up_a[j], NT)).astype(bf)
            grads[j] = rg
            terms = [mm(lg_up, xr, TN), mm(low_up, pg, TN), mm(lg_dn, hidden, TN), mm(low_dn, scaled, TN)]
            used = sum(v.shape[1] for v in terms)
            n_part, cols = n_dp // local, acc.shape[2]
            if n_part * cols > used:
                terms.append(jnp.zeros((acc.shape[1], n_part * cols - used), f32))
            terms = jnp.concatenate(terms, axis=1)
            for q in range(n_part):
                acc[j * n_part + q] += adapter_scale * terms[:, q * cols : (q + 1) * cols]
            for i in range(len(pieces)):
                back = jnp.sum(picks[i, j] * slot_gate[i * SLOTS : (i + 1) * SLOTS], axis=0, keepdims=True)
                for b in range(2):
                    gates[i][b] += hits[i, j][b] * back[:, b * rows : (b + 1) * rows]
        for i, p in enumerate(pieces):
            pick = jnp.concatenate([picks[i, j].astype(bf) for j in range(local)], axis=0)
            grad = jnp.concatenate(
                [grads[j][i * SLOTS : (i + 1) * SLOTS] for j in range(local)], axis=0
            )
            part[pl.ds(2 * p, 2)] = mm(pick, grad, TN).astype(bf).reshape(2, rows, width)
            for b in range(2):
                gate[b, p] = jnp.concatenate(
                    [gates[i][b], jnp.zeros((16 - top, rows), f32)], axis=0
                ).astype(bf)

    for ci in range(6):
        hop(ci, 0, first=True).start()
    for t in range(3):
        own_to_mate(t).start()
        own_copy(t).start()
    before[...] = (
        lax.broadcasted_iota(jnp.int32, (piece, piece), 0)
        < lax.broadcasted_iota(jnp.int32, (piece, piece), 1)
    ).astype(bf)
    acc[...] = jnp.zeros_like(acc)
    for t in range(3):
        own_copy(t).wait()
        own_to_mate(t).wait_recv()
    far = n // 2
    everyone = list(range(6))
    move(1, everyone, reach(2))

    def round_(s, _):
        move(s, everyone, everyone)
        for ci in range(6):
            to_mate(ci, s - 1).wait_recv()
        compute([at(s - 1), at(1 - s)])
        return 0

    lax.fori_loop(2, far - 1, round_, 0)
    for s in range(max(far - 1, 2), far + 1):
        move(s, reach(s), reach(s + 1))
        for ci in range(6):
            to_mate(ci, s - 1).wait_recv()
        if s < far:
            compute([at(s - 1), at(1 - s)])
    for ci in reach(far):
        to_mate(ci, far).wait_recv()

    def last(g, _):
        compute([at(-g), at(lax.rem(g, far))])
        return 0

    lax.fori_loop(far - 1, far + 1, last, 0)

    first, second, ring, pair = [], [], {}, {}
    for k in range(1, n_dp):
        first.append(dma(acc.at[gat(k)], got.at[k], send1.at[k], recv1.at[k], "dp", gat(k)))
        first[-1].start()

    def sum_parts():
        total = acc[group]
        for k in range(1, n_dp):
            first[k - 1].wait_recv()
            total = total + got[k]
        added[...] = total.astype(bf)
        for k in range(1, n_dp):
            second.append(dma(added, summed.at[group], send2.at[k], recv2.at[k], "dp", gat(k)))
            second[-1].start()
        summed[group] = total.astype(bf)

    half = part.shape[1] // 2
    spans = (pl.ds(0, half), pl.ds(half, half), slice(None))
    sends, recvs = (sa, sb, sg), (ra, rb, rg)

    order = [n // 2]
    for k in range(n // 2 - 1, 0, -1):
        order += [k, n - k]
    order.append(0)
    gcopy = dma(gate.at[1 - core], mg, psend.at[n], precv.at[n], "expert", mate)
    gcopy.start()
    for k in order:
        pair[k] = dma(
            part.at[at(k) * 2 + 1 - core], mp.at[at(k)], psend.at[k], precv.at[k], "expert", mate
        )
        pair[k].start()
    arrived = set()

    def mine(t, k):
        if t == 2:
            if "g" not in arrived:
                gcopy.wait_recv()
                arrived.add("g")
            return gate[core, at(k)].astype(jnp.float32) + mg[at(k)].astype(jnp.float32)
        if k not in arrived:
            pair[k].wait_recv()
            arrived.add(k)
        return part[at(k) * 2 + core, spans[t]].astype(jnp.float32) + mp[at(k), spans[t]].astype(
            jnp.float32
        )

    for s in range(n // 2):
        if s == min(3, n // 2 - 1):
            sum_parts()
        for ci, (t, d, hops) in enumerate(chains):
            if s >= hops:
                continue
            total = mine(t, (d * (hops - s)) % n)
            slot = 0 if d > 0 else 1
            if s > 0:
                ring[ci, s - 1].wait_recv()
                total = total + recvs[t][slot, s - 1].astype(jnp.float32)
            sends[t][slot, s] = total.astype(jnp.bfloat16)
            ring[ci, s] = dma(
                sends[t].at[slot, s], recvs[t].at[slot, s], send.at[ci, s], recv.at[ci, s],
                "expert", at(d) * 2 + core,
            )
            ring[ci, s].start()
    for t in range(3):
        total = mine(t, 0)
        for ci, (u, d, hops) in enumerate(chains):
            if u == t:
                ring[ci, hops - 1].wait_recv()
                total = total + recvs[t][0 if d > 0 else 1, hops - 1].astype(jnp.float32)
        if t == 2:
            gout[...] = total.astype(jnp.bfloat16)
        else:
            out[spans[t]] = total.astype(jnp.bfloat16)
    for copy in ring.values():
        copy.wait_send()
    for copy in pair.values():
        copy.wait_send()
    gcopy.wait_send()
    for copy in first:
        copy.wait_send()
    for copy in second:
        copy.wait()
    for ci, (_, _, hops) in enumerate(chains):
        for s in range(hops):
            hop(ci, s, first=s == 0).wait_send()
            to_mate(ci, s + 1).wait_send()
    for t in range(3):
        own_to_mate(t).wait_send()


def shards(tokens, cotangent, expert_ids, gate_weights, up_w, up_a, up_b, dn_w, dn_a, dn_b):
    bf, f32 = jnp.bfloat16, jnp.float32
    n_dev = lax.axis_size("expert")
    n_dp = lax.axis_size("dp")
    n = n_dev // 2
    local, width, ff = up_w.shape
    rank = up_a.shape[2]
    rows, top = expert_ids.shape
    used = 2 * (width + ff)
    n_part = n_dp // local
    cols = -(-used // (n_part * 128)) * 128

    meta = jnp.concatenate([expert_ids.T.astype(bf), gate_weights.T], axis=0)
    meta = jnp.pad(meta, ((0, 16 - 2 * top), (0, 0)))
    half = (2, n // 2, rows // 2, width)
    dma_sem = pltpu.SemaphoreType.DMA
    vmem = pltpu.VMEM
    input_grad, gate_grad, summed = pl.pallas_call(
        functools.partial(step_kernel, n, n_dp, top),
        out_shape=[
            jax.ShapeDtypeStruct((rows, width), bf),
            jax.ShapeDtypeStruct((16, rows), bf),
            jax.ShapeDtypeStruct((n_dp, rank, cols), bf),
        ],
        in_specs=[pl.BlockSpec(memory_space=vmem)] * 9,
        out_specs=[pl.BlockSpec(memory_space=vmem)] * 3,
        scratch_shapes=[
            vmem((n_dev, rows, width), bf),
            vmem((n_dev, rows, width), bf),
            vmem((n_dev, 16, rows), bf),
            vmem((2 * rows, 2 * rows), bf),
            vmem((n_dev, rows, width), bf),
            vmem((2, n, 16, rows), bf),
            vmem((n, rows, width), bf),
            vmem((n, 16, rows), bf),
            vmem(half, bf),
            vmem(half, bf),
            vmem(half, bf),
            vmem(half, bf),
            vmem((2, n // 2, 16, rows), bf),
            vmem((2, n // 2, 16, rows), bf),
            vmem((n_dp, rank, cols), f32),
            vmem((n_dp, rank, cols), f32),
            vmem((rank, cols), bf),
            dma_sem((6, n // 2)),
            dma_sem((6, n // 2)),
            dma_sem((6, n // 2 + 1)),
            dma_sem((6, n // 2 + 1)),
            dma_sem((3,)),
            dma_sem((6, n // 2)),
            dma_sem((6, n // 2)),
            dma_sem((n + 1,)),
            dma_sem((n + 1,)),
            dma_sem((n_dp,)),
            dma_sem((n_dp,)),
            dma_sem((n_dp,)),
            dma_sem((n_dp,)),
        ],
        compiler_params=pltpu.CompilerParams(
            collective_id=0, has_side_effects=True, vmem_limit_bytes=62 * 1024 * 1024
        ),
    )(tokens, cotangent, meta, up_w, up_a, up_b, dn_w, dn_a, dn_b)
    full = summed.reshape(local, n_part, rank, cols).swapaxes(1, 2).reshape(local, rank, -1)
    au, bu, ad, bd = jnp.split(full[:, :, :used], [width, width + ff, width + 2 * ff], axis=2)
    return (
        input_grad,
        gate_grad[:top].T,
        au.transpose(0, 2, 1),
        bu,
        ad.transpose(0, 2, 1),
        bd,
    )


def solution(mesh):
    rows = P(("dp", "expert"), None)
    experts = P("expert", None, None)
    return jax.shard_map(
        shards,
        mesh=mesh,
        in_specs=(rows,) * 4 + (experts,) * 6,
        out_specs=(rows,) * 2 + (experts,) * 4,
        check_vma=False,
    )
```

```python
import functools

import jax
import jax.numpy as jnp
from jax import lax
from jax.experimental import pallas as pl
from jax.experimental.pallas import tpu as pltpu
from jax.sharding import PartitionSpec as P

adapter_scale = 2.0
PIECE_BLOCKS = 2
SLOTS = 48


def mm(a, b, dims):
    return lax.dot_general(a, b, (dims, ((), ())), preferred_element_type=jnp.float32)


NN = ((1,), (0,))
NT = ((1,), (1,))
TN = ((0,), (0,))


def dma(src, dst, send, recv, axis, index):
    return pltpu.make_async_remote_copy(
        src_ref=src,
        dst_ref=dst,
        send_sem=send,
        recv_sem=recv,
        device_id={axis: index},
        device_id_type=pl.DeviceIdType.MESH,
    )


def greet(peers):
    barrier = pltpu.get_barrier_semaphore()
    for axis, peer in peers:
        pl.semaphore_signal(
            barrier, inc=1, device_id={axis: peer}, device_id_type=pl.DeviceIdType.MESH
        )
    pl.semaphore_wait(barrier, len(peers))


def ring_place(n):
    me = lax.axis_index("expert")
    z, core = me // 2, lax.rem(me, 2)
    at = lambda off: lax.rem(z + off + 2 * n, n)
    return me, z, core, at


def ring_chains(n, tensors):
    far, near = n // 2, n - 1 - n // 2
    chains = []
    for t in range(tensors):
        chains.append((t, 1, far if t != 1 else near))
        chains.append((t, -1, near if t != 1 else far))
    return chains


def step_kernel(n, n_dp, top, x, c, m, up_w, up_a, up_b, dn_w, dn_a, dn_b, out, gout, summed,
                xo, co, mo, before, part, gate, mp, mg, sa, ra, sb, rb, sg, rg, acc, got, added,
                gsend, grecv, gpsend, gprecv, own, send, recv, psend, precv, send1, recv1, send2, recv2):
    bf, f32 = jnp.bfloat16, jnp.float32
    me, z, core, at = ring_place(n)
    mate = z * 2 + 1 - core
    group = lax.axis_index("dp")
    gat = lambda off: lax.rem(group + off + n_dp, n_dp)
    greet(
        [("expert", at(1) * 2 + core), ("expert", at(-1) * 2 + core), ("expert", mate)]
        + [("dp", gat(k)) for k in range(1, n_dp)]
    )
    chains = ring_chains(n, 3)
    local = up_w.shape[0]
    rows, width = x.shape
    piece = PIECE_BLOCKS * rows

    ins, outs = (x, c, m), (xo, co, mo)

    def hop(ci, s, first=False):
        t, d, _ = chains[ci]
        block = at(-d * s) * 2 + core
        return dma(
            ins[t] if first else outs[t].at[block], outs[t].at[block],
            gsend.at[ci, s], grecv.at[ci, s], "expert", at(d) * 2 + core,
        )

    def to_mate(ci, s):
        t, d, _ = chains[ci]
        block = at(-d * s) * 2 + core
        return dma(
            outs[t].at[block], outs[t].at[block],
            gpsend.at[ci, s], gprecv.at[ci, s], "expert", mate,
        )

    def own_to_mate(t):
        return dma(ins[t], outs[t].at[me], gpsend.at[2 * t, 0], gprecv.at[2 * t, 0], "expert", mate)

    def own_copy(t):
        return pltpu.make_async_copy(ins[t], outs[t].at[me], own.at[t])

    def move(s, active, forward):
        for ci in active:
            hop(ci, s - 1).wait_recv()
            if ci in forward:
                hop(ci, s).start()
            to_mate(ci, s).start()

    def reach(s):
        return [ci for ci, (_, _, hops) in enumerate(chains) if hops >= s]

    def compute(pieces):
        picks, hits, gate_rows = {}, {}, {}
        blocks = {}
        for i, p in enumerate(pieces):
            blocks[i] = [mo[2 * p + b].astype(f32) for b in range(2)]
            for j in range(local):
                e = (me * local + j).astype(f32)
                hits[i, j] = [(v[:top] == e).astype(f32) for v in blocks[i]]
                mask = jnp.concatenate(
                    [jnp.sum(h, axis=0, keepdims=True) for h in hits[i, j]], axis=1
                )
                weight = jnp.concatenate(
                    [
                        jnp.sum(h * v[top : 2 * top], axis=0, keepdims=True)
                        for h, v in zip(hits[i, j], blocks[i])
                    ],
                    axis=1,
                )
                place = mm(jnp.broadcast_to(mask, (8, piece)).astype(bf), before[...], NN)[:1]
                slot = lax.broadcasted_iota(jnp.int32, (SLOTS, piece), 0).astype(f32)
                pick = jnp.where(slot == place, jnp.broadcast_to(mask, (SLOTS, piece)), 0.0)
                gate_rows[i, j] = jnp.sum(pick * weight, axis=1, keepdims=True)
                picks[i, j] = pick
        grads = {}
        gates = [[0.0, 0.0] for _ in pieces]

        def take(source, j):
            return jnp.concatenate(
                [
                    mm(picks[i, j].astype(bf), source[pl.ds(2 * p, 2)].reshape(piece, width), NN)
                    for i, p in enumerate(pieces)
                ],
                axis=0,
            )

        for j in range(local):
            xr = take(xo, j).astype(bf)
            cf = take(co, j)
            low_up = mm(xr, up_a[j], NT).astype(bf)
            pre = mm(xr, up_w[j], NN) + adapter_scale * mm(low_up, up_b[j], NN)
            s = jax.nn.sigmoid(pre)
            hidden = (pre * s).astype(bf)
            low_dn = mm(hidden, dn_a[j], NT).astype(bf)
            res = mm(hidden, dn_w[j], NN) + adapter_scale * mm(low_dn, dn_b[j], NN)
            slot_gate = jnp.sum(res * cf, axis=1, keepdims=True).astype(bf).astype(f32)
            weight = jnp.concatenate([gate_rows[i, j] for i in range(len(pieces))], axis=0)
            scaled = (weight * cf).astype(bf)
            lg_dn = mm(scaled, dn_b[j], NT).astype(bf)
            hg = mm(scaled, dn_w[j], NT) + adapter_scale * mm(lg_dn, dn_a[j], NN)
            pg = (hg * (s * (1.0 + pre * (1.0 - s)))).astype(bf)
            lg_up = mm(pg, up_b[j], NT).astype(bf)
            rg = (mm(pg, up_w[j], NT) + adapter_scale * mm(lg_up, up_a[j], NN)).astype(bf)
            grads[j] = rg
            terms = [mm(lg_up, xr, TN), mm(low_up, pg, TN), mm(lg_dn, hidden, TN), mm(low_dn, scaled, TN)]
            used = sum(v.shape[1] for v in terms)
            n_part, cols = n_dp // local, acc.shape[2]
            if n_part * cols > used:
                terms.append(jnp.zeros((acc.shape[1], n_part * cols - used), f32))
            terms = jnp.concatenate(terms, axis=1)
            for q in range(n_part):
                acc[j * n_part + q] += adapter_scale * terms[:, q * cols : (q + 1) * cols]
            for i in range(len(pieces)):
                back = jnp.sum(picks[i, j] * slot_gate[i * SLOTS : (i + 1) * SLOTS], axis=0, keepdims=True)
                for b in range(2):
                    gates[i][b] += hits[i, j][b] * back[:, b * rows : (b + 1) * rows]
        for i, p in enumerate(pieces):
            pick = jnp.concatenate([picks[i, j].astype(bf) for j in range(local)], axis=0)
            grad = jnp.concatenate(
                [grads[j][i * SLOTS : (i + 1) * SLOTS] for j in range(local)], axis=0
            )
            part[pl.ds(2 * p, 2)] = mm(pick, grad, TN).astype(bf).reshape(2, rows, width)
            for b in range(2):
                gate[b, p] = jnp.concatenate(
                    [gates[i][b], jnp.zeros((16 - top, rows), f32)], axis=0
                ).astype(bf)

    for ci in range(6):
        hop(ci, 0, first=True).start()
    for t in range(3):
        own_to_mate(t).start()
        own_copy(t).start()
    before[...] = (
        lax.broadcasted_iota(jnp.int32, (piece, piece), 0)
        < lax.broadcasted_iota(jnp.int32, (piece, piece), 1)
    ).astype(bf)
    acc[...] = jnp.zeros_like(acc)
    for t in range(3):
        own_copy(t).wait()
        own_to_mate(t).wait_recv()
    far = n // 2
    everyone = list(range(6))

    def pair(k):
        return dma(
            part.at[at(k) * 2 + 1 - core], mp.at[at(k)], psend.at[k], precv.at[k], "expert", mate
        )

    compute([z])
    pair(0).start()

    def work(s):
        for ci in everyone:
            to_mate(ci, s).wait_recv()
        compute([at(s), at(-s)])
        pair(s).start()
        pair(n - s).start()

    def round_(s, _):
        move(s, everyone, everyone)
        work(s)
        return 0

    lax.fori_loop(1, far - 1, round_, 0)
    move(far - 1, everyone, reach(far))
    work(far - 1)
    move(far, reach(far), [])
    first, second, ring, arrived = [], [], {}, set()
    def sum_parts():
        total = acc[group]
        for k in range(1, n_dp):
            first[k - 1].wait_recv()
            total = total + got[k]
        added[...] = total.astype(bf)
        for k in range(1, n_dp):
            second.append(dma(added, summed.at[group], send2.at[k], recv2.at[k], "dp", gat(k)))
            second[-1].start()
        summed[group] = total.astype(bf)

    half = part.shape[1] // 2
    spans = (pl.ds(0, half), pl.ds(half, half), slice(None))
    sends, recvs = (sa, sb, sg), (ra, rb, rg)

    gcopy = dma(gate.at[1 - core], mg, psend.at[n], precv.at[n], "expert", mate)

    def mine(t, k):
        if t == 2:
            if "g" not in arrived:
                gcopy.wait_recv()
                arrived.add("g")
            return gate[core, at(k)].astype(jnp.float32) + mg[at(k)].astype(jnp.float32)
        if k not in arrived:
            pair(k).wait_recv()
            arrived.add(k)
        return part[at(k) * 2 + core, spans[t]].astype(jnp.float32) + mp[at(k), spans[t]].astype(
            jnp.float32
        )

    def add_and_send(ci, s):
        t, d, hops = chains[ci]
        total = mine(t, (d * (hops - s)) % n)
        slot = 0 if d > 0 else 1
        if s > 0:
            ring[ci, s - 1].wait_recv()
            total = total + recvs[t][slot, s - 1].astype(jnp.float32)
        sends[t][slot, s] = total.astype(jnp.bfloat16)
        ring[ci, s] = dma(
            sends[t].at[slot, s], recvs[t].at[slot, s], send.at[ci, s], recv.at[ci, s],
            "expert", at(d) * 2 + core,
        )
        ring[ci, s].start()

    early = [ci for ci, (t, _, hops) in enumerate(chains) if t < 2 and hops < far]
    for ci in early:
        add_and_send(ci, 0)
    for ci in reach(far):
        to_mate(ci, far).wait_recv()
    compute([at(far)])
    pair(far).start()
    gcopy.start()

    for k in range(1, n_dp):
        first.append(dma(acc.at[gat(k)], got.at[k], send1.at[k], recv1.at[k], "dp", gat(k)))
        first[-1].start()


    for s in range(far):
        if s == min(3, far - 1):
            sum_parts()
        for ci, (_, _, hops) in enumerate(chains):
            if s < hops and not (s == 0 and ci in early):
                add_and_send(ci, s)
    for t in range(3):
        total = mine(t, 0)
        for ci, (u, d, hops) in enumerate(chains):
            if u == t:
                ring[ci, hops - 1].wait_recv()
                total = total + recvs[t][0 if d > 0 else 1, hops - 1].astype(jnp.float32)
        if t == 2:
            gout[...] = total.astype(jnp.bfloat16)
        else:
            out[spans[t]] = total.astype(jnp.bfloat16)
    for copy in ring.values():
        copy.wait_send()
    for k in range(n):
        pair(k).wait_send()
    gcopy.wait_send()
    for copy in first:
        copy.wait_send()
    for copy in second:
        copy.wait()
    for ci, (_, _, hops) in enumerate(chains):
        for s in range(hops):
            hop(ci, s, first=s == 0).wait_send()
            to_mate(ci, s + 1).wait_send()
    for t in range(3):
        own_to_mate(t).wait_send()


def shards(tokens, cotangent, expert_ids, gate_weights, up_w, up_a, up_b, dn_w, dn_a, dn_b):
    bf, f32 = jnp.bfloat16, jnp.float32
    n_dev = lax.axis_size("expert")
    n_dp = lax.axis_size("dp")
    n = n_dev // 2
    local, width, ff = up_w.shape
    rank = up_a.shape[2]
    rows, top = expert_ids.shape
    used = 2 * (width + ff)
    n_part = n_dp // local
    cols = -(-used // (n_part * 128)) * 128

    meta = jnp.concatenate([expert_ids.T.astype(bf), gate_weights.T], axis=0)
    meta = jnp.pad(meta, ((0, 16 - 2 * top), (0, 0)))
    half = (2, n // 2, rows // 2, width)
    dma_sem = pltpu.SemaphoreType.DMA
    vmem = pltpu.VMEM
    input_grad, gate_grad, summed = pl.pallas_call(
        functools.partial(step_kernel, n, n_dp, top),
        out_shape=[
            jax.ShapeDtypeStruct((rows, width), bf),
            jax.ShapeDtypeStruct((16, rows), bf),
            jax.ShapeDtypeStruct((n_dp, rank, cols), bf),
        ],
        in_specs=[pl.BlockSpec(memory_space=vmem)] * 9,
        out_specs=[pl.BlockSpec(memory_space=vmem)] * 3,
        scratch_shapes=[
            vmem((n_dev, rows, width), bf),
            vmem((n_dev, rows, width), bf),
            vmem((n_dev, 16, rows), bf),
            vmem((2 * rows, 2 * rows), bf),
            vmem((n_dev, rows, width), bf),
            vmem((2, n, 16, rows), bf),
            vmem((n, rows, width), bf),
            vmem((n, 16, rows), bf),
            vmem(half, bf),
            vmem(half, bf),
            vmem(half, bf),
            vmem(half, bf),
            vmem((2, n // 2, 16, rows), bf),
            vmem((2, n // 2, 16, rows), bf),
            vmem((n_dp, rank, cols), f32),
            vmem((n_dp, rank, cols), f32),
            vmem((rank, cols), bf),
            dma_sem((6, n // 2)),
            dma_sem((6, n // 2)),
            dma_sem((6, n // 2 + 1)),
            dma_sem((6, n // 2 + 1)),
            dma_sem((3,)),
            dma_sem((6, n // 2)),
            dma_sem((6, n // 2)),
            dma_sem((n + 1,)),
            dma_sem((n + 1,)),
            dma_sem((n_dp,)),
            dma_sem((n_dp,)),
            dma_sem((n_dp,)),
            dma_sem((n_dp,)),
        ],
        compiler_params=pltpu.CompilerParams(
            collective_id=0, has_side_effects=True, vmem_limit_bytes=62 * 1024 * 1024
        ),
    )(
        tokens, cotangent, meta, up_w, up_a.transpose(0, 2, 1), up_b,
        dn_w, dn_a.transpose(0, 2, 1), dn_b,
    )
    full = summed.reshape(local, n_part, rank, cols).swapaxes(1, 2).reshape(local, rank, -1)
    au, bu, ad, bd = jnp.split(full[:, :, :used], [width, width + ff, width + 2 * ff], axis=2)
    return (
        input_grad,
        gate_grad[:top].T,
        au.transpose(0, 2, 1),
        bu,
        ad.transpose(0, 2, 1),
        bd,
    )


def solution(mesh):
    rows = P(("dp", "expert"), None)
    experts = P("expert", None, None)
    return jax.shard_map(
        shards,
        mesh=mesh,
        in_specs=(rows,) * 4 + (experts,) * 6,
        out_specs=(rows,) * 2 + (experts,) * 4,
        check_vma=False,
    )
```
